32 devices in a mesh: shard: 4 (over y, core), ctx: 2 (over x), tp: 4 (over z).
Axes of the slice: x: 2, y: 2, z: 4, core: 2. Of those that a mesh axis runs over, the one named last changes fastest.
Arguments:
- tokens: bfloat16 [4, 1500, 768], P('shard', 'ctx'), may hold values from -8 to 8
- w_qkv: bfloat16 [768, 3, 768], P('shard', None, 'tp'), may hold values from -2 to 2
- b_qv: bfloat16 [2, 768], P(None, ('tp', 'shard')), may hold values from -3 to 3
- w_out: bfloat16 [768, 768], P('tp', 'shard'), may hold values from -1.5 to 1.5
- b_out: bfloat16 [768], P('shard'), may hold values from -2 to 2
- w_fc1: bfloat16 [768, 3072], P('shard', 'tp'), may hold values from -0.21875 to 0.21875
- b_fc1: bfloat16 [3072], P(('tp', 'shard')), may hold values from -3 to 3
- w_fc2: bfloat16 [3072, 768], P('tp', 'shard'), may hold values from -0.109375 to 0.109375
- b_fc2: bfloat16 [768], P('shard'), may hold values from -2 to 2
- ln1_gain: bfloat16 [768], P('shard'), may hold values from 0.25 to 1.75
- ln1_bias: bfloat16 [768], P('shard'), may hold values from -2 to 2
- ln2_gain: bfloat16 [768], P('shard'), may hold values from 0.25 to 1.75
- ln2_bias: bfloat16 [768], P('shard'), may hold values from -2 to 2
- cotangent: bfloat16 [4, 1500, 768], P('shard', 'ctx'), may hold values from -6 to 6
Outputs:
- output: bfloat16 [4, 1500, 768], P('shard', 'ctx')
- grad_tokens: bfloat16 [4, 1500, 768], P('shard', 'ctx')
- grad_w_qkv: float32 [768, 3, 768], P('shard', None, 'tp')
- grad_b_qv: float32 [2, 768], P(None, ('tp', 'shard'))
- grad_w_out: float32 [768, 768], P('tp', 'shard')
- grad_b_out: float32 [768], P('shard')
- grad_w_fc1: float32 [768, 3072], P('shard', 'tp')
- grad_b_fc1: float32 [3072], P(('tp', 'shard'))
- grad_w_fc2: float32 [3072, 768], P('tp', 'shard')
- grad_b_fc2: float32 [768], P('shard')
- grad_ln1_gain: float32 [768], P('shard')
- grad_ln1_bias: float32 [768], P('shard')
- grad_ln2_gain: float32 [768], P('shard')
- grad_ln2_bias: float32 [768], P('shard')
The draws below stay inside these ranges and needn't reach their ends.
All inputs are finite; a program needn't handle non-finite values.
Results may differ from the reference program's by a relative error of at most 0.024.
Values may be sent and summed in bfloat16 or wider, within the bound.
No kernel may reach another device: no remote copies, remote signals or barrier semaphores. Data moves between devices by JAX's collectives and lax.ppermute only.
A program may use at most 128 MiB of HBM per device.

```python
import math
import jax
import jax.numpy as jnp
from jax import lax

D = 768
FF = 3072
HEAD_DIM = 64
FRAMES = 1500
CLIPS = 4


def draw_tokens(key, part):
    first_key = jax.random.fold_in(key, 0)
    values = jax.random.normal(first_key, (CLIPS, FRAMES, D), jnp.float32)
    return jnp.clip(values, -8.0, 8.0).astype(jnp.bfloat16)


def draw_w_qkv(key, part):
    subkeys = jax.random.split(key, 1)
    stacked = jax.random.normal(subkeys[0], (D, 3, D), jnp.float32) / math.sqrt(D)
    return jnp.clip(stacked, -2.0, 2.0).astype(jnp.bfloat16)


def shard_levels(rng, shape, pieces, least, largest):
    def one(position, blocks):
        draws = jax.random.uniform(jax.random.fold_in(jax.random.fold_in(rng, 6), position), (blocks,), jnp.float32, least / len(pieces), largest / len(pieces))
        return jnp.repeat(jnp.exp(draws), shape[position] // blocks).reshape((-1,) + (1,) * (len(shape) - position - 1))

    gain = one(*pieces[0])
    for cut in pieces[1:]:
        gain = gain * one(*cut)
    return gain


def normal_values(rng, shape, scale, limit, shards=(), kind=jnp.bfloat16):
    drawn = jax.random.normal(rng, shape, jnp.float32) * scale
    if len(shards) > 0:
        drawn = shard_levels(rng, shape, shards, -0.22, 0.18) * drawn
    return jnp.clip(drawn, min=-limit, max=limit).astype(kind)


def setup_inputs(seed: int = 0) -> dict:
    key_list = jax.random.split(jax.random.key(seed), 15)
    return {
        "tokens": draw_tokens(jax.random.fold_in(key_list[14], 71), 0),
        "w_qkv": draw_w_qkv(jax.random.fold_in(key_list[14], 71), 0),
        "b_qv": normal_values(key_list[2], (2, D), 0.5, 3.0, ((1, 16),)),
        "w_out": normal_values(key_list[3], (D, D), 16 ** -0.5, 1.5, ((0, 4), (1, 4))),
        "b_out": normal_values(key_list[4], (D,), 0.3, 2.0, ((0, 4),)),
        "w_fc1": normal_values(key_list[5], (D, FF), D ** -0.5, 0.21875, ((0, 4), (1, 4))),
        "b_fc1": normal_values(key_list[6], (FF,), 0.5, 3.0, ((0, 16),)),
        "w_fc2": normal_values(key_list[7], (FF, D), FF ** -0.5, 0.109375, ((0, 4), (1, 4))),
        "b_fc2": normal_values(key_list[8], (D,), 0.3, 2.0, ((0, 4),)),
        "ln1_gain": jnp.clip(1.0 + 0.15 * jax.random.normal(key_list[9], (D,), jnp.float32), 0.25, 1.75).astype(jnp.bfloat16),
        "ln1_bias": normal_values(key_list[10], (D,), 0.3, 2.0, ((0, 4),)),
        "ln2_gain": jnp.clip(1.0 + 0.15 * jax.random.normal(key_list[11], (D,), jnp.float32), 0.25, 1.75).astype(jnp.bfloat16),
        "ln2_bias": normal_values(key_list[12], (D,), 0.3, 2.0, ((0, 4),)),
        "cotangent": normal_values(key_list[13], (CLIPS, FRAMES, D), 1.0, 6.0, ((0, 4), (1, 2))),
    }


@jax.custom_vjp
def low(v):
    return lax.optimization_barrier(v.astype(jnp.bfloat16)).astype(jnp.float32)

@jax.custom_vjp
def low_back(v):
    return v

def low_keep(v):
    return (low(v), None)

def low_pass(kept, grad):
    return (grad,)

def back_keep(v):
    return (v, None)

def back_low(kept, grad):
    return (low(grad),)
low.defvjp(low_keep, low_pass)
low_back.defvjp(back_keep, back_low)

def product(left, right, form):
    return jnp.einsum(form, left, right, precision=lax.Precision.HIGHEST)

def norm_rows(rows, gain_vec, bias_vec):
    row_mean = lax.optimization_barrier(jnp.mean(rows, axis=-1, keepdims=True))
    centred = rows - row_mean
    variance = lax.optimization_barrier(jnp.mean(centred * centred, axis=-1, keepdims=True))
    return centred * lax.rsqrt(variance + 1e-05) * gain_vec + bias_vec

def clip_forward(params, frames_in):
    w_qkv, b_qv, w_out, b_out, w_fc1, b_fc1, w_fc2, b_fc2, ln1_gain, ln1_bias, ln2_gain, ln2_bias = params
    head_count = D // HEAD_DIM
    normed_one = low(norm_rows(frames_in, ln1_gain, ln1_bias))
    zero_row = jnp.zeros_like(b_qv[0])
    bias_table = jnp.stack([b_qv[0], zero_row, b_qv[1]], axis=0)
    projected = product(normed_one, w_qkv, 'fd,dtk->ftk') + bias_table
    projected = low(low_back(projected))
    queries = projected[:, 0].reshape(FRAMES, head_count, HEAD_DIM)
    keys_all = projected[:, 1].reshape(FRAMES, head_count, HEAD_DIM)
    values_all = projected[:, 2].reshape(FRAMES, head_count, HEAD_DIM)
    scores = low_back(product(queries, keys_all, 'fhc,ghc->hfg') * 0.125)
    probabilities = jax.nn.softmax(scores, axis=-1)
    attended = product(low(probabilities), values_all, 'hfg,ghc->fhc').reshape(FRAMES, D)
    attended = low(low_back(attended))
    branch = low_back(product(attended, w_out, 'fk,kd->fd') + b_out)
    middle = frames_in + branch
    normed_two = low(norm_rows(middle, ln2_gain, ln2_bias))
    hidden_pre = low_back(product(normed_two, w_fc1, 'fd,dh->fh') + b_fc1)
    activated = low(jax.nn.gelu(hidden_pre, approximate=False))
    mixed = low_back(product(activated, w_fc2, 'fh,hd->fd') + b_fc2)
    return middle + mixed

def forward(params, tokens):
    checked = jax.checkpoint(clip_forward)
    return lax.map(lambda frames_in: checked(params, frames_in), tokens)

def reference(tokens, w_qkv, b_qv, w_out, b_out, w_fc1, b_fc1, w_fc2, b_fc2, ln1_gain, ln1_bias, ln2_gain, ln2_bias, cotangent):
    params = tuple((item.astype(jnp.float32) for item in (w_qkv, b_qv, w_out, b_out, w_fc1, b_fc1, w_fc2, b_fc2, ln1_gain, ln1_bias, ln2_gain, ln2_bias)))
    inputs = tokens.astype(jnp.float32)
    result, pullback = jax.vjp(forward, params, inputs)
    grad_params, grad_inputs = pullback(cotangent.astype(jnp.float32))
    return (result.astype(jnp.bfloat16), grad_inputs.astype(jnp.bfloat16), grad_params[0], grad_params[1], grad_params[2], grad_params[3], grad_params[4], grad_params[5], grad_params[6], grad_params[7], grad_params[8], grad_params[9], grad_params[10], grad_params[11])
```

```python
import functools

import jax
import jax.numpy as jnp
from jax import lax
from jax.experimental import pallas as pl
from jax.experimental.pallas import tpu as pltpu
from jax.sharding import PartitionSpec as P

HEAD_DIM = 64
TILE = 256
BF = jnp.bfloat16
F32 = jnp.float32


def dot(left, right, dims=((1,), (0,))):
    return lax.dot_general(left, right, (dims, ((), ())), preferred_element_type=F32)


NT = ((1,), (1,))
TN = ((0,), (0,))


def normalized(rows):
    mean = jnp.mean(rows, axis=-1, keepdims=True)
    centred = rows - mean
    variance = jnp.mean(centred * centred, axis=-1, keepdims=True)
    rstd = lax.rsqrt(variance + 1e-05)
    return centred * rstd, rstd


def first_norm_kernel(count, take, own, other, gain, bias, picked, normed):
    rows = jnp.where(take[0] == 0, own[...], other[...])
    index = pl.program_id(0) * TILE + lax.broadcasted_iota(jnp.int32, rows.shape, 0)
    rows = jnp.where(index < count, rows.astype(F32), 0.0)
    picked[...] = rows.astype(BF)
    xhat, _ = normalized(rows)
    normed[...] = (xhat * gain[...] + bias[...]).astype(BF)


def first_norm(take, own, other, gain, bias, padded):
    count, width = own.shape
    row = pl.BlockSpec((TILE, width), lambda i, t: (i, 0))
    vec = pl.BlockSpec((1, width), lambda i, t: (0, 0))
    return pl.pallas_call(
        functools.partial(first_norm_kernel, count),
        grid_spec=pltpu.PrefetchScalarGridSpec(
            num_scalar_prefetch=1,
            grid=(padded // TILE,),
            in_specs=[row, row, vec, vec],
            out_specs=[row, row],
        ),
        out_shape=[jax.ShapeDtypeStruct((padded, width), BF)] * 2,
        name="first_norm",
    )(take, own, other, gain, bias)


def head_blocks(tensor_t, heads):
    row_head = lax.broadcasted_iota(jnp.int32, tensor_t.shape, 0) // HEAD_DIM
    zero = jnp.zeros_like(tensor_t)
    return jnp.concatenate([jnp.where(row_head == h, tensor_t, zero) for h in range(heads)], axis=1)


def row_blocks(tensor, heads):
    lane_head = lax.broadcasted_iota(jnp.int32, tensor.shape, 1) // HEAD_DIM
    zero = jnp.zeros_like(tensor)
    return jnp.concatenate([jnp.where(lane_head == h, tensor, zero) for h in range(heads)], axis=0)


def turned(tensor):
    return jnp.transpose(tensor.astype(F32), (1, 0)).astype(tensor.dtype)


def attention_forward_kernel(first, frames, heads, *refs):
    if first:
        queries, keys, acc_out, stat_out, values_t = refs
    else:
        queries, keys, acc_in, stat_in, attended_t, exact_t, stat_out, values_t = refs
    width = heads * HEAD_DIM
    padded = keys.shape[0]

    @pl.when(pl.program_id(0) == 0)
    def _():
        values_t[...] = turned(keys[:, width:])

    scores = dot(keys[:, :width], head_blocks(turned(queries[...]), heads))
    row = lax.broadcasted_iota(jnp.int32, scores.shape, 0)
    scores = jnp.where(row < frames, scores, -1e30)
    top = jnp.max(scores, axis=0, keepdims=True)
    if not first:
        old_top = stat_in[0, 0:1, :]
        top = jnp.maximum(top, old_top)
    weight = jnp.exp(scores - top)
    total = jnp.sum(weight, axis=0, keepdims=True)
    if not first:
        scale = jnp.exp(old_top - top)
        total = total + scale * stat_in[0, 1:2, :]
    weight = weight.astype(BF)
    if first:
        for h in range(heads):
            span = slice(h * HEAD_DIM, (h + 1) * HEAD_DIM)
            acc_out[span, :] = dot(values_t[span, :], weight[:, h * TILE : (h + 1) * TILE])
        stat_out[0, 0:1, :] = top
        stat_out[0, 1:2, :] = total
    else:
        inverse = 1.0 / total
        for h in range(heads):
            span = slice(h * HEAD_DIM, (h + 1) * HEAD_DIM)
            cols = slice(h * TILE, (h + 1) * TILE)
            value = dot(values_t[span, :], weight[:, cols]) + scale[:, cols] * acc_in[span, :]
            value = value * inverse[:, cols]
            exact_t[span, :] = value
            attended_t[span, :] = value.astype(BF)
        stat_out[0, 0:1, :] = top + jnp.log(total)


def attention_forward(frames, queries, keys, partial=None):
    padded, width = queries.shape
    heads = width // HEAD_DIM
    tiles = padded // TILE
    first = partial is None
    q_spec = pl.BlockSpec((TILE, width), lambda i: (i, 0))
    k_spec = pl.BlockSpec((padded, 2 * width), lambda i: (0, 0))
    t_spec = pl.BlockSpec((width, TILE), lambda i: (0, i))
    s_spec = pl.BlockSpec((1, 8, heads * TILE), lambda i: (i, 0, 0))
    stat = jax.ShapeDtypeStruct((tiles, 8, heads * TILE), F32)
    turned_f32 = jax.ShapeDtypeStruct((width, padded), F32)
    turned_bf = jax.ShapeDtypeStruct((width, padded), BF)
    return pl.pallas_call(
        functools.partial(attention_forward_kernel, first, frames, heads),
        grid=(tiles,),
        in_specs=[q_spec, k_spec] + ([] if first else [t_spec, s_spec]),
        out_specs=[t_spec, s_spec] if first else [t_spec, t_spec, s_spec],
        out_shape=[turned_f32, stat] if first else [turned_bf, turned_f32, stat],
        scratch_shapes=[pltpu.VMEM((width, padded), BF)],
        name="attention_forward_own" if first else "attention_forward_other",
    )(queries, keys, *([] if first else partial))


def attention_backward_kernel(first, frames, heads, *refs):
    if first:
        queries, keys, grad_out, exact_t, stat, grad_q_t, grad_kv, grad_acc, keys_t = refs
    else:
        queries, keys, grad_out, exact_t, stat, grad_q_in, received, grad_q, grad_kv, grad_acc, keys_t = refs
    width = heads * HEAD_DIM
    step = pl.program_id(0)

    @pl.when(step == 0)
    def _():
        keys_t[...] = turned(keys[:, :width])
        grad_acc[...] = jnp.zeros_like(grad_acc)

    go_t = turned(grad_out[...])
    product = go_t.astype(F32) * exact_t[...]
    delta = jnp.concatenate(
        [
            jnp.sum(product[h * HEAD_DIM : (h + 1) * HEAD_DIM], axis=0, keepdims=True)
            for h in range(heads)
        ],
        axis=1,
    )
    scores = dot(keys[:, :width], head_blocks(turned(queries[...]), heads))
    row = lax.broadcasted_iota(jnp.int32, scores.shape, 0)
    weight = jnp.where(row < frames, jnp.exp(scores - stat[0, 0:1, :]), 0.0)
    grad_weight = dot(keys[:, width:], head_blocks(go_t, heads))
    grad_scores = (weight * (grad_weight - delta)).astype(BF)
    grad_acc[:, width:] += dot(weight.astype(BF), row_blocks(grad_out[...], heads))
    grad_acc[:, :width] += dot(grad_scores, row_blocks(queries[...], heads))
    pieces = [
        dot(keys_t[h * HEAD_DIM : (h + 1) * HEAD_DIM, :], grad_scores[:, h * TILE : (h + 1) * TILE])
        for h in range(heads)
    ]
    grad_q_tile = jnp.concatenate(pieces, axis=0)
    if first:
        grad_q_t[...] = grad_q_tile
    else:
        grad_q[...] = jnp.transpose((grad_q_tile + grad_q_in[...]) * 0.125, (1, 0)).astype(BF)

    @pl.when(step == pl.num_programs(0) - 1)
    def _():
        grad_kv[...] = grad_acc[...].astype(grad_kv.dtype)


def attention_backward(frames, queries, keys, grad_out, exact_t, stat, grad_q_t=None):
    padded, width = queries.shape
    heads = width // HEAD_DIM
    tiles = padded // TILE
    first = grad_q_t is None
    q_spec = pl.BlockSpec((TILE, width), lambda i: (i, 0))
    k_spec = pl.BlockSpec((padded, 2 * width), lambda i: (0, 0))
    t_spec = pl.BlockSpec((width, TILE), lambda i: (0, i))
    s_spec = pl.BlockSpec((1, 8, heads * TILE), lambda i: (i, 0, 0))
    grad_q_shape = (
        jax.ShapeDtypeStruct((width, padded), F32)
        if first
        else jax.ShapeDtypeStruct((padded, width), BF)
    )

    def kernel(*refs):
        if not first:
            refs = refs[:6] + (None,) + refs[6:]
        attention_backward_kernel(first, frames, heads, *refs)

    return pl.pallas_call(
        kernel,
        grid=(tiles,),
        in_specs=[q_spec, k_spec, q_spec, t_spec, s_spec] + ([] if first else [t_spec]),
        out_specs=[t_spec if first else q_spec, k_spec],
        out_shape=[grad_q_shape, jax.ShapeDtypeStruct((padded, 2 * width), BF if first else F32)],
        scratch_shapes=[
            pltpu.VMEM((padded, 2 * width), F32),
            pltpu.VMEM((width, padded), BF),
        ],
        name="attention_backward_other" if first else "attention_backward_own",
    )(queries, keys, grad_out, exact_t, stat, *([] if first else [grad_q_t]))


def feed_kernel(parts, *refs):
    att = refs[:parts]
    w_out = refs[parts : 2 * parts]
    tokens, vectors, w_one, b_one, w_two_t, cotangent = refs[2 * parts : 2 * parts + 6]
    middle, normed, active, grad_pre, grad_part, bias_sum = refs[2 * parts + 6 :]
    branch = dot(att[0][...], w_out[0][...], TN)
    for i in range(1, parts):
        branch = branch + dot(att[i][...], w_out[i][...], TN)
    mid = tokens[...].astype(F32) + (branch + vectors[2:3, :])
    middle[...] = mid
    xhat, _ = normalized(mid)
    second = (xhat * vectors[3:4, :] + vectors[4:5, :]).astype(BF)
    normed[...] = second
    hidden = dot(second, w_one[...]) + b_one[...]
    cumulative = 0.5 * (1.0 + lax.erf(hidden * 0.7071067811865476))
    active[...] = (hidden * cumulative).astype(BF)
    slope = cumulative + hidden * (jnp.exp(-0.5 * hidden * hidden) * 0.3989422804014327)
    pre = (dot(cotangent[...], w_two_t[...]) * slope).astype(BF)
    grad_pre[...] = pre
    grad_part[...] = dot(pre, w_one[...], NT).astype(BF)

    @pl.when(pl.program_id(0) == 0)
    def _():
        bias_sum[...] = jnp.zeros_like(bias_sum)

    bias_sum[0:1, :] += jnp.sum(pre.astype(F32), axis=0, keepdims=True)


def feed(att, w_out, tokens, vectors, w_one, b_one, w_two_t, cotangent):
    padded, width = tokens.shape
    slab, inner = att[0].shape[0], w_one.shape[1]
    row = pl.BlockSpec((TILE, width), lambda i: (i, 0))
    wide = pl.BlockSpec((TILE, inner), lambda i: (i, 0))

    def whole(array):
        return pl.BlockSpec(array.shape, lambda i: (0,) * array.ndim)

    return pl.pallas_call(
        functools.partial(feed_kernel, len(att)),
        grid=(padded // TILE,),
        in_specs=[pl.BlockSpec((slab, TILE), lambda i: (0, i))] * len(att)
        + [whole(w) for w in w_out]
        + [row, whole(vectors), whole(w_one), whole(b_one), whole(w_two_t), row],
        out_specs=[row, row, wide, wide, row, pl.BlockSpec((8, inner), lambda i: (0, 0))],
        out_shape=[
            jax.ShapeDtypeStruct((padded, width), F32),
            jax.ShapeDtypeStruct((padded, width), BF),
            jax.ShapeDtypeStruct((padded, inner), BF),
            jax.ShapeDtypeStruct((padded, inner), BF),
            jax.ShapeDtypeStruct((padded, width), BF),
            jax.ShapeDtypeStruct((8, inner), F32),
        ],
        name="feed_forward_and_back",
    )(*att, *w_out, tokens, vectors, w_one, b_one, w_two_t, cotangent)


def norm_back_kernel(second, place, own, near, far, rows, gain, carried, *outs):
    grad = own[...].astype(F32) + near[...].astype(F32) + far[...].astype(F32)
    xhat, rstd = normalized(rows[...].astype(F32))
    weighted = grad * gain[...]
    inner = weighted - jnp.mean(weighted, axis=-1, keepdims=True)
    inner = inner - xhat * jnp.mean(weighted * xhat, axis=-1, keepdims=True)
    base = carried[...].astype(F32)
    result = base + rstd * inner
    sums = outs[-1]
    sums[...] = jnp.zeros_like(sums)
    sums[0:1, :] = jnp.sum(grad * xhat, axis=0, keepdims=True)
    sums[1:2, :] = jnp.sum(grad, axis=0, keepdims=True)
    if second:
        outs[0][...] = result
        rounded = result.astype(BF)
        outs[1][...] = rounded
        sums[2:3, :] = jnp.sum(rounded.astype(F32), axis=0, keepdims=True)
        sums[3:4, :] = jnp.sum(base, axis=0, keepdims=True)
    else:
        outs[0][...] = result.astype(BF)


def norm_back(second, place, own, near, far, rows, gain, carried):
    quarter, width = far.shape
    pick = pl.BlockSpec((quarter, width), lambda i, p: (p[0], 0))
    pick_half = pl.BlockSpec((quarter, width), lambda i, p: (p[1], 0))
    whole = pl.BlockSpec((quarter, width), lambda i, p: (0, 0))
    vec = pl.BlockSpec((1, width), lambda i, p: (0, 0))
    outs = [jax.ShapeDtypeStruct((quarter, width), F32), jax.ShapeDtypeStruct((quarter, width), BF)]
    if not second:
        outs = outs[1:]
    return pl.pallas_call(
        functools.partial(norm_back_kernel, second),
        grid_spec=pltpu.PrefetchScalarGridSpec(
            num_scalar_prefetch=1,
            grid=(1,),
            in_specs=[pick, pick_half, whole, pick, vec, pick if second else whole],
            out_specs=[whole] * len(outs) + [pl.BlockSpec((8, width), lambda i, p: (0, 0))],
        ),
        out_shape=outs + [jax.ShapeDtypeStruct((8, width), F32)],
        name="second_norm_back" if second else "first_norm_back",
    )(place, own, near, far, rows, gain, carried)


class Links:
    def __init__(self, mesh):
        self.n_shard, self.n_tp = mesh.shape["shard"], mesh.shape["tp"]
        assert self.n_tp == 4 and mesh.shape["ctx"] == 2
        assert self.n_shard >= 2 and self.n_shard & (self.n_shard - 1) == 0
        self.s = lax.axis_index("shard")
        self.z = lax.axis_index("tp")
        self.k = self.s & 1
        self.low, self.high = self.z & 1, self.z >> 1
        self.r = self.low + 2 * self.k
        self.home = self.k == self.high

    def shard_bit(self, x, bit):
        return lax.ppermute(x, "shard", [(i, i ^ bit) for i in range(self.n_shard)])

    def core(self, x):
        return self.shard_bit(x, 1)

    def tp_bit(self, x, bit):
        return lax.ppermute(x, "tp", [(i, i ^ bit) for i in range(self.n_tp)])

    def other_half(self, x):
        return lax.ppermute(x, "ctx", [(0, 1), (1, 0)])

    def shard_bits(self):
        return [b for b in (1 << i for i in range(1, self.n_shard.bit_length())) if b < self.n_shard]

    @staticmethod
    def ordered(bit, mine, other, axis=0):
        low = jnp.where(bit == 0, mine, other)
        high = jnp.where(bit == 0, other, mine)
        return jnp.concatenate([low, high], axis=axis)

    def gather_rows(self, block):
        received = self.tp_bit(block, 2)
        keep = jnp.where(self.home, block, received)
        give = jnp.where(self.home, received, block)
        rows = self.ordered(self.k, keep, self.core(give))
        for bit in self.shard_bits():
            rows = self.ordered(self.s & bit, rows, self.shard_bit(rows, bit))
        return rows

    def scatter_rows(self, grad):
        for bit in reversed(self.shard_bits()):
            half = grad.shape[0] // 2
            mine_high = (self.s & bit) != 0
            low, high = grad[:half], grad[half:]
            give = jnp.where(mine_high, low, high).astype(BF)
            keep = jnp.where(mine_high, high, low)
            grad = keep.astype(F32) + self.shard_bit(give, bit).astype(F32)
        half = grad.shape[0] // 2
        grad = grad.astype(BF)
        low, high = grad[:half], grad[half:]
        keep = jnp.where(self.k == 0, low, high)
        got = self.core(jnp.where(self.k == 0, high, low))
        mine = jnp.where(self.home, keep, got)
        away = self.tp_bit(jnp.where(self.home, got, keep), 2)
        mine = (mine.astype(F32) + away.astype(F32)).astype(BF)
        return mine.astype(F32) + self.other_half(mine).astype(F32)

    def gather_group(self, quarter):
        half = self.ordered(self.low, quarter, self.tp_bit(quarter, 1))
        return self.ordered(self.k, half, self.core(half))

    def scatter_group(self, partial):
        half = partial.shape[0] // 2
        quarter = half // 2
        give = lax.dynamic_slice_in_dim(partial, (1 - self.k) * half, half, 0)
        near = self.core(give)
        away = (1 - self.low) * quarter
        send = lax.dynamic_slice_in_dim(partial, self.k * half + away, quarter, 0).astype(F32)
        send = send + lax.dynamic_slice_in_dim(near, away, quarter, 0).astype(F32)
        return partial, near, self.tp_bit(send.astype(BF), 1)

    def broadcast_home(self, quarter):
        pieces = []
        for d in range(4):
            pairs = []
            for s in range(self.n_shard):
                for z in range(self.n_tp):
                    r = (z & 1) + 2 * (s & 1)
                    pairs.append((s * self.n_tp + z, (s - (s & 1) + (z >> 1)) * self.n_tp + (r ^ d)))
            pieces.append(lax.ppermute(quarter, ("shard", "tp"), pairs))
        low = self.ordered(self.low, pieces[0], pieces[1])
        high = self.ordered(self.low, pieces[2], pieces[3])
        return self.ordered(self.high, low, high)


def per_device(
    mesh,
    tokens,
    w_qkv,
    b_qv,
    w_out,
    b_out,
    w_fc1,
    b_fc1,
    w_fc2,
    b_fc2,
    ln1_gain,
    ln1_bias,
    ln2_gain,
    ln2_bias,
    cotangent,
):
    links = Links(mesh)
    clips, frames, width = tokens.shape
    assert clips == 1
    padded = -(-frames // TILE) * TILE
    assert padded % 64 == 0
    n_shard = links.n_shard
    block, slab, inner = w_qkv.shape[0], w_qkv.shape[2], w_fc1.shape[1]

    own_tokens, own_cotangent = tokens[0], cotangent[0]
    sent_tokens = links.core(own_tokens)
    key_value = jnp.concatenate([w_qkv[:, 1], w_qkv[:, 2]], axis=1)
    query_out = jnp.concatenate([w_qkv[:, 0], w_out.T], axis=1)
    rows_kv = links.gather_rows(key_value)

    small = jnp.concatenate(
        [ln1_gain, ln1_bias, b_out, ln2_gain, ln2_bias, b_fc2, b_qv.reshape(-1), b_fc1]
    )[None]
    small = jnp.stack([small, links.tp_bit(small, 2)], axis=0)
    small = links.ordered(links.k, small, links.core(small), axis=1)
    for bit in links.shard_bits():
        small = links.ordered(links.s & bit, small, links.shard_bit(small, bit), axis=1)
    small = small.astype(F32)
    vectors = small[0, :, : 6 * block].reshape(n_shard, 6, block)
    vectors = vectors.transpose(1, 0, 2).reshape(6, width)
    vectors = jnp.concatenate([vectors, jnp.zeros((2, width), F32)], axis=0)
    mine = jnp.where(links.home, small[0], small[1])
    part = b_qv.shape[1]
    bias_qv = mine[:, 6 * block : 6 * block + 2 * part].reshape(n_shard, 2, part)
    bias_qv = bias_qv.transpose(1, 0, 2).reshape(2, slab)
    bias_one = mine[:, 6 * block + 2 * part :].reshape(1, inner)

    rows_qo = links.gather_rows(query_out)
    sent_cotangent = links.core(own_cotangent)
    rows_one = links.gather_rows(w_fc1)
    rows_two_t = links.gather_rows(w_fc2.T)

    take = jnp.where(links.home, 0, 1).astype(jnp.int32)[None]
    picked, normed_one = first_norm(
        take, own_tokens, sent_tokens, vectors[0:1], vectors[1:2], padded
    )
    kv_bias = jnp.concatenate([jnp.zeros((slab,), F32), bias_qv[1]])
    keys = (dot(normed_one, rows_kv) + kv_bias).astype(BF)
    other_keys = links.other_half(keys)
    rows_q, rows_o_t = rows_qo[:, :slab], rows_qo[:, slab:]
    queries = ((dot(normed_one, rows_q) + bias_qv[0]).astype(BF) * 0.125).astype(BF)

    partial = attention_forward(frames, queries, keys)
    attended_t, exact_t, stat = attention_forward(frames, queries, other_keys, partial)
    rows_o = rows_o_t.T
    near_o = links.tp_bit(rows_o, 1)
    out_weights = [rows_o, near_o, links.core(rows_o), links.core(near_o)]
    near_att = links.tp_bit(attended_t, 1)
    attended = [attended_t, near_att, links.core(attended_t), links.core(near_att)]

    grad_result = jnp.where(links.home, own_cotangent, sent_cotangent)
    grad_result = jnp.pad(grad_result, ((0, padded - frames), (0, 0)))
    middle, normed_two, activated, grad_pre, grad_two_part, grad_b1 = feed(
        attended, out_weights, picked, vectors, rows_one, bias_one, rows_two_t, grad_result
    )
    quarter = padded // 4
    place = jnp.stack([links.r, links.low]).astype(jnp.int32)
    own, near, far = links.scatter_group(grad_two_part)
    cot_quarter = lax.dynamic_slice_in_dim(grad_result, links.r * quarter, quarter, 0)
    grad_middle, branch_quarter, sums_two = norm_back(
        True, place, own, near, far, middle, vectors[3:4], grad_result
    )
    grad_branch = links.gather_group(branch_quarter)
    grad_attended = dot(grad_branch, rows_o_t).astype(BF)

    grad_q_t, grad_other = attention_backward(
        frames, queries, other_keys, grad_attended, exact_t, stat
    )
    returned = links.other_half(grad_other)
    grad_q, grad_own = attention_backward(
        frames, queries, keys, grad_attended, exact_t, stat, grad_q_t
    )
    grad_kv = (grad_own + returned.astype(F32)).astype(BF)
    grad_one_part = (dot(grad_kv, rows_kv, NT) + dot(grad_q, rows_q, NT)).astype(BF)
    own, near, far = links.scatter_group(grad_one_part)
    token_quarter, sums_one = norm_back(
        False, place, own, near, far, picked, vectors[0:1], grad_middle
    )
    grad_tokens = links.broadcast_home(token_quarter)[None, :frames]

    mlp_part = dot(activated, rows_two_t, NT).astype(BF)
    own, near, far = links.scatter_group(mlp_part)
    mlp = lax.dynamic_slice_in_dim(own, links.r * quarter, quarter, 0).astype(F32)
    mlp = mlp + lax.dynamic_slice_in_dim(near, links.low * quarter, quarter, 0).astype(F32)
    mlp = mlp + far.astype(F32)
    middle_quarter = lax.dynamic_slice_in_dim(middle, links.r * quarter, quarter, 0)
    out_quarter = (middle_quarter + (mlp + vectors[5:6])).astype(BF)
    output = links.broadcast_home(out_quarter)[None, :frames]

    slice_two = links.scatter_rows(dot(grad_result, activated, TN)).T
    slice_one = links.scatter_rows(dot(normed_two, grad_pre, TN))
    slice_out = links.scatter_rows(dot(grad_branch, attended_t, ((0,), (1,)))).T
    slice_kv = links.scatter_rows(dot(normed_one, grad_kv, TN))
    slice_q = links.scatter_rows(dot(normed_one, grad_q, TN))
    slice_qkv = jnp.stack([slice_q, slice_kv[:, :slab], slice_kv[:, slab:]], axis=1)

    bias_q = jnp.sum(grad_q.astype(F32), axis=0)
    bias_v = jnp.sum(grad_kv[:, slab:].astype(F32), axis=0)
    mine = jnp.concatenate([grad_b1[0], bias_q, bias_v])
    slots = jnp.where(jnp.arange(4)[:, None] == links.r, mine[None], 0.0)
    flat = jnp.concatenate([sums_one[:2].reshape(-1), sums_two[:4].reshape(-1), slots.reshape(-1)])
    flat = lax.psum(flat, ("shard", "ctx", "tp"))
    vector_sums = flat[: 6 * width].reshape(6, width)
    vector_sums = lax.dynamic_slice_in_dim(vector_sums, links.s * block, block, 1)
    slots = flat[6 * width :].reshape(4, inner + 2 * slab)
    slots = lax.dynamic_slice_in_dim(slots, links.z, 1, 0)[0]
    sum_one = lax.dynamic_slice_in_dim(slots[:inner], links.s * b_fc1.shape[0], b_fc1.shape[0], 0)
    sum_qv = lax.dynamic_slice_in_dim(slots[inner:].reshape(2, slab), links.s * part, part, 1)
    return (
        output,
        grad_tokens,
        slice_qkv,
        sum_qv,
        slice_out,
        vector_sums[4],
        slice_one,
        sum_one,
        slice_two,
        vector_sums[5],
        vector_sums[0],
        vector_sums[1],
        vector_sums[2],
        vector_sums[3],
    )


def solution(mesh):
    placed = (
        P("shard", "ctx", None),
        P("shard", None, "tp"),
        P(None, ("tp", "shard")),
        P("tp", "shard"),
        P("shard"),
        P("shard", "tp"),
        P(("tp", "shard")),
        P("tp", "shard"),
        P("shard"),
        P("shard"),
        P("shard"),
        P("shard"),
        P("shard"),
        P("shard", "ctx", None),
    )
    return jax.shard_map(
        functools.partial(per_device, mesh),
        mesh=mesh,
        in_specs=placed,
        out_specs=(
            P("shard", "ctx", None),
            P("shard", "ctx", None),
            P("shard", None, "tp"),
            P(None, ("tp", "shard")),
            P("tp", "shard"),
            P("shard"),
            P("shard", "tp"),
            P(("tp", "shard")),
            P("tp", "shard"),
            P("shard"),
            P("shard"),
            P("shard"),
            P("shard"),
            P("shard"),
        ),
        check_vma=False,
    )
```
